32 devices in a mesh: dp: 16 (over z, y, core), tensor: 2 (over x).
Axes of the slice: x: 2, y: 2, z: 4, core: 2. Of those that a mesh axis runs over, the one named last changes fastest.
Arguments:
- tokens: bfloat16 [32768, 1024], P(('dp', 'tensor')), may hold values from -6 to 6
- gain_one: float32 [1024], replicated, may hold values from 0.5 to 1.5
- gain_two: float32 [1024], replicated, may hold values from 0.5 to 1.5
- w_query: bfloat16 [1024, 1024], P(None, 'tensor'), may hold values from -0.1875 to 0.1875
- w_key: bfloat16 [512, 1024], P('tensor'), may hold values from -0.1875 to 0.1875
- w_value: bfloat16 [512, 1024], P('tensor'), may hold values from -0.1875 to 0.1875
- w_out: bfloat16 [1024, 1024], P('tensor'), may hold values from -1 to 1
- w_gate: bfloat16 [32, 512, 1024], P(None, 'tensor'), may hold values from -0.1875 to 0.1875
- w_up: bfloat16 [32, 512, 1024], P(None, 'tensor'), may hold values from -0.1875 to 0.1875
- w_down: bfloat16 [32, 512, 1024], P(None, 'tensor'), may hold values from -1 to 1
- slot_index: int32 [16, 32, 640], P('dp'), may hold values from 0 to 2047, as said below
- slot_gate: float32 [16, 32, 640], P('dp'), may hold values from 0 to 0.19, as said below
- grad_output: bfloat16 [32768, 1024], P(('dp', 'tensor')), may hold values from -6 to 6
Outputs:
- output: bfloat16 [32768, 1024], P(('dp', 'tensor'))
- grad_tokens: bfloat16 [32768, 1024], P('dp')
- grad_gain_one: float32 [1024], replicated
- grad_gain_two: float32 [1024], replicated
- grad_w_query: float32 [1024, 1024], P(None, 'tensor')
- grad_w_key: float32 [512, 1024], P('tensor')
- grad_w_value: float32 [512, 1024], P('tensor')
- grad_w_out: float32 [1024, 1024], P('tensor')
- grad_w_gate: float32 [32, 512, 1024], P(None, 'tensor')
- grad_w_up: float32 [32, 512, 1024], P(None, 'tensor')
- grad_w_down: float32 [32, 512, 1024], P(None, 'tensor')
The draws below stay inside these ranges and needn't reach their ends.
Inputs may be any that keep to these rules, and one draw needn't show every extreme that they name: `slot_index`: in each sequence group the 640 slots of one expert name distinct tokens of that group. `slot_gate`: in each expert's block the live slots (gate above zero) come first, followed by empty slots of gate zero; a block has 320 to 640 live slots, and in every sequence group some block is full.
All inputs are finite; a program needn't handle non-finite values.
Results may differ from the reference program's by a relative error of at most 0.023.
Values may be sent and summed in bfloat16 or wider, within the bound.
No kernel may reach another device: no remote copies, remote signals or barrier semaphores. Data moves between devices by JAX's collectives and lax.ppermute only.
A program may use at most 448 MiB of HBM per device.

```python
import jax
import jax.numpy as jnp
from jax import lax

D = 1024
QH = 16
KVH = 8
HD = 64
EXPERTS = 32
FFE = 512
SEQ_LEN = 1024
GROUPS = 16
TOKG = 2048
TOKENS = 32768
CAP = 640


def live_counts(key):
    first, second = jax.random.split(jax.random.fold_in(key, 7))
    counts = jax.random.randint(first, (GROUPS, EXPERTS), CAP // 2, CAP + 1)
    fullest = jax.random.randint(second, (GROUPS, 1), 0, EXPERTS)
    return jnp.where(jnp.arange(EXPERTS)[None, :] == fullest, CAP, counts)


def pick_slots(single_key):
    return jax.random.permutation(single_key, TOKG)[:CAP]


def draw_slot_index(key, part):
    key_list = jax.random.split(jax.random.fold_in(key, 3), GROUPS * EXPERTS)
    picked = jax.vmap(pick_slots)(key_list)
    return picked.reshape(GROUPS, EXPERTS, CAP).astype(jnp.int32)


def draw_slot_gate(key, part):
    counts = live_counts(key)
    values = jax.random.uniform(jax.random.fold_in(key, 5), (GROUPS, EXPERTS, CAP), jnp.float32, 0.06, 0.19)
    is_live = jnp.arange(CAP)[None, None, :] < counts[:, :, None]
    return jnp.where(is_live, values, 0.0).astype(jnp.float32)


def block_scale(rng, extent, pieces, least, top_value):
    factor_of, own = 1.0, jax.random.fold_in(rng, 6)
    for axis_at, blocks in pieces:
        draws = jnp.exp(jax.random.uniform(jax.random.fold_in(own, axis_at), (blocks,), jnp.float32, least / len(pieces), top_value / len(pieces)))
        factor_of = factor_of * jnp.repeat(draws, extent[axis_at] // blocks).reshape([-1 if axis == axis_at else 1 for axis in range(len(extent))])
    return factor_of


def centred(key, shape, scale, limit, cuts=(), kind=jnp.bfloat16):
    level = block_scale(key, shape, cuts, -0.22, 0.18) if cuts else 1.0
    drawn = jax.random.normal(key, shape, jnp.float32) * scale * level
    return jnp.minimum(jnp.maximum(drawn, -limit), limit).astype(kind)


def setup_inputs(seed: int = 0) -> dict:
    splits = jax.random.split(jax.random.key(seed), 14)
    return {
        "tokens": centred(splits[0], (TOKENS, D), 1.0, 6.0, ((0, 32),)),
        "gain_one": jnp.clip(1.0 + 0.1 * jax.random.normal(splits[1], (D,), jnp.float32), 0.5, 1.5),
        "gain_two": jnp.clip(1.0 + 0.1 * jax.random.normal(splits[2], (D,), jnp.float32), 0.5, 1.5),
        "w_query": centred(splits[3], (D, QH * HD), D ** -0.5, 0.1875, ((1, 2),)),
        "w_key": centred(splits[4], (KVH * HD, D), D ** -0.5, 0.1875, ((0, 2),)),
        "w_value": centred(splits[5], (KVH * HD, D), D ** -0.5, 0.1875, ((0, 2),)),
        "w_out": centred(splits[6], (QH * HD, D), (QH * HD // 32) ** -0.5, 1.0, ((0, 2),)),
        "w_gate": centred(splits[7], (EXPERTS, FFE, D), D ** -0.5, 0.1875, ((1, 2),)),
        "w_up": centred(splits[8], (EXPERTS, FFE, D), D ** -0.5, 0.1875, ((1, 2),)),
        "w_down": centred(splits[9], (EXPERTS, FFE, D), (FFE // 16) ** -0.5, 1.0, ((1, 2),)),
        "slot_index": draw_slot_index(jax.random.fold_in(splits[13], 71), 0),
        "slot_gate": draw_slot_gate(jax.random.fold_in(splits[13], 71), 0),
        "grad_output": centred(splits[12], (TOKENS, D), 1.0, 6.0, ((0, 32),)),
    }


EPS = 1e-05
THETA = 10000.0
MASKED = -1e+30
HIGH = lax.Precision.HIGHEST

@jax.custom_vjp
def low(v):
    return lax.optimization_barrier(v.astype(jnp.bfloat16)).astype(jnp.float32)

@jax.custom_vjp
def low_back(v):
    return v

def low_keep(v):
    return (low(v), None)

def low_pass(kept, grad):
    return (grad,)

def back_keep(v):
    return (v, None)

def back_low(kept, grad):
    return (low(grad),)
low.defvjp(low_keep, low_pass)
low_back.defvjp(back_keep, back_low)

def normalize(values, gain):
    return values * lax.rsqrt(lax.optimization_barrier(jnp.mean(values * values, axis=-1, keepdims=True)) + EPS) * gain

def rope_tables(row_count, head_size):
    position = (jnp.arange(row_count) % SEQ_LEN).astype(jnp.float32)
    exponent = jnp.arange(head_size // 2).astype(jnp.float32) * (2.0 / head_size)
    angles = position[:, None] * jnp.power(THETA, -exponent)[None, :]
    return (jnp.cos(angles)[:, None, :], jnp.sin(angles)[:, None, :])

def rotate(values, cosine, sine_tab):
    half_size = values.shape[-1] // 2
    first, second = (values[..., :half_size], values[..., half_size:])
    return jnp.concatenate([first * cosine - second * sine_tab, second * cosine + first * sine_tab], axis=-1)

def attend(members):
    queries, keys, values = members
    length = queries.shape[0]
    score_scale = queries.shape[-1] ** (-0.5)
    scores = low_back(jnp.einsum('qgrd,kgd->grqk', queries, keys, precision=HIGH) * score_scale)
    causal = lax.broadcasted_iota(jnp.int32, (length, length), 1) <= lax.broadcasted_iota(jnp.int32, (length, length), 0)
    weights = low(jax.nn.softmax(jnp.where(causal, scores, MASKED), axis=-1))
    return low(low_back(jnp.einsum('grqk,kgd->qgrd', weights, values, precision=HIGH)))

def layer_block(rows_in, gain_one, gain_two, w_query, w_key, w_value, w_out, w_gate, w_up, w_down, slot_rows, slot_weight):
    row_count, width = rows_in.shape
    cosine, sine_tab = rope_tables(row_count, HD)
    normed_one = low(normalize(rows_in, gain_one))
    queries = low_back(jnp.dot(normed_one, w_query, precision=HIGH, preferred_element_type=jnp.float32))
    keys = low_back(jnp.dot(normed_one, w_key.T, precision=HIGH, preferred_element_type=jnp.float32))
    values = low(low_back(jnp.dot(normed_one, w_value.T, precision=HIGH, preferred_element_type=jnp.float32)))
    queries = low(rotate(queries.reshape(row_count, QH, HD), cosine, sine_tab))
    keys = low(rotate(keys.reshape(row_count, KVH, HD), cosine, sine_tab))
    seq_count = row_count // SEQ_LEN
    mixed = lax.map(jax.checkpoint(attend), (queries.reshape(seq_count, SEQ_LEN, KVH, QH // KVH, HD), keys.reshape(seq_count, SEQ_LEN, KVH, HD), values.reshape(seq_count, SEQ_LEN, KVH, HD)))
    mixed = mixed.reshape(row_count, QH * HD)
    residual = rows_in + low_back(jnp.dot(mixed, w_out, precision=HIGH, preferred_element_type=jnp.float32))
    normed_two = low(normalize(residual, gain_two))
    gathered = normed_two[slot_rows]
    gate_pre = low_back(jnp.einsum('ecd,efd->ecf', gathered, w_gate, precision=HIGH))
    up_pre = low_back(jnp.einsum('ecd,efd->ecf', gathered, w_up, precision=HIGH))
    active = low(jax.nn.silu(gate_pre) * up_pre)
    expert_out = low_back(jnp.einsum('ecf,efd->ecd', active, w_down, precision=HIGH)) * slot_weight[..., None]
    mixture = jnp.zeros_like(residual).at[slot_rows.reshape(-1)].add(expert_out.reshape(-1, width))
    return residual + low_back(mixture)

def reference(tokens, gain_one, gain_two, w_query, w_key, w_value, w_out, w_gate, w_up, w_down, slot_index, slot_gate, grad_output):
    params = (gain_one.astype(jnp.float32), gain_two.astype(jnp.float32), w_query.astype(jnp.float32), w_key.astype(jnp.float32), w_value.astype(jnp.float32), w_out.astype(jnp.float32), w_gate.astype(jnp.float32), w_up.astype(jnp.float32), w_down.astype(jnp.float32))
    inputs = tokens.astype(jnp.float32).reshape(GROUPS, TOKG, D)
    cotangent = grad_output.astype(jnp.float32).reshape(GROUPS, TOKG, D)

    def one_group(running, members):
        rows_in, slot_rows, slot_weight, grad_rows = members

        def forward(rows_value, *weights):
            return layer_block(rows_value, *weights, slot_rows, slot_weight)
        result, pullback = jax.vjp(forward, rows_in, *params)
        grad_list = pullback(grad_rows)
        running = tuple((summed + group_part for summed, group_part in zip(running, grad_list[1:])))
        return (running, (result, grad_list[0]))
    start = tuple((jnp.zeros_like(param_val) for param_val in params))
    sums, (results, input_grads) = lax.scan(one_group, start, (inputs, slot_index, slot_gate.astype(jnp.float32), cotangent))
    return (results.reshape(TOKENS, D).astype(jnp.bfloat16), input_grads.reshape(TOKENS, D).astype(jnp.bfloat16), sums[0], sums[1], sums[2], sums[3], sums[4], sums[5], sums[6], sums[7], sums[8])
```

```python
import math

import jax
import jax.numpy as jnp
from jax import lax
from jax.experimental import pallas as pl
from jax.experimental.pallas import tpu as pltpu
from jax.sharding import PartitionSpec as P

HD = 64
SEQ_LEN = 1024


EPS = 1e-05
THETA = 10000.0
MASKED = -1e30


def rope_tables(row_count, head_size):
    position = (jnp.arange(row_count) % SEQ_LEN).astype(jnp.float32)
    exponent = jnp.arange(head_size // 2).astype(jnp.float32) * (2.0 / head_size)
    angles = position[:, None] * jnp.power(THETA, -exponent)[None, :]
    return (jnp.cos(angles)[:, None, :], jnp.sin(angles)[:, None, :])


def rotate(values, cosine, sine_tab):
    half_size = values.shape[-1] // 2
    first, second = (values[..., :half_size], values[..., half_size:])
    return jnp.concatenate(
        [first * cosine - second * sine_tab, second * cosine + first * sine_tab], axis=-1
    )


def unrotate(grads_in, cosine, sine_tab):
    half_size = grads_in.shape[-1] // 2
    first, second = (grads_in[..., :half_size], grads_in[..., half_size:])
    return jnp.concatenate(
        [first * cosine + second * sine_tab, second * cosine - first * sine_tab], axis=-1
    )


def normalize(values, gain):
    inverse = lax.rsqrt(jnp.mean(values * values, axis=-1, keepdims=True) + EPS)
    return (values * inverse * gain, inverse)


def norm_back(values, inverse, gain, grad_normed):
    scaled = grad_normed * gain
    return inverse * scaled - values * inverse**3 * jnp.mean(
        scaled * values, axis=-1, keepdims=True
    )


def causal_mask(length):
    query_pos = lax.broadcasted_iota(jnp.int32, (length, length), 0)
    key_pos = lax.broadcasted_iota(jnp.int32, (length, length), 1)
    return key_pos <= query_pos


def attend_forward(members):
    queries, keys, values = members
    score_scale = queries.shape[-1] ** (-0.5)
    scores = (
        jnp.einsum("qgrd,kgd->grqk", queries, keys, preferred_element_type=jnp.float32)
        * score_scale
    )
    scores = jnp.where(causal_mask(queries.shape[0]), scores, MASKED)
    row_peak = jnp.max(scores, axis=-1, keepdims=True)
    exponent = jnp.exp(scores - row_peak)
    row_total = jnp.sum(exponent, axis=-1, keepdims=True)
    weights = (exponent / row_total).astype(jnp.bfloat16)
    mixed = jnp.einsum(
        "grqk,kgd->qgrd", weights, values, preferred_element_type=jnp.float32
    ).astype(jnp.bfloat16)
    return (mixed, row_peak[..., 0] + jnp.log(row_total[..., 0]))


def attend_backward(members):
    queries, keys, values, grad_mixed, log_total = members
    score_scale = queries.shape[-1] ** (-0.5)
    scores = (
        jnp.einsum("qgrd,kgd->grqk", queries, keys, preferred_element_type=jnp.float32)
        * score_scale
    )
    scores = jnp.where(causal_mask(queries.shape[0]), scores, MASKED)
    weights = jnp.exp(scores - log_total[..., None])
    grad_weights = jnp.einsum(
        "qgrd,kgd->grqk", grad_mixed, values, preferred_element_type=jnp.float32
    )
    grad_values = jnp.einsum(
        "grqk,qgrd->kgd",
        weights.astype(jnp.bfloat16),
        grad_mixed,
        preferred_element_type=jnp.float32,
    )
    row_delta = jnp.sum(grad_weights * weights, axis=-1, keepdims=True)
    grad_scores = (weights * (grad_weights - row_delta)).astype(jnp.bfloat16)
    grad_queries = (
        jnp.einsum("grqk,kgd->qgrd", grad_scores, keys, preferred_element_type=jnp.float32)
        * score_scale
    )
    grad_keys = (
        jnp.einsum("grqk,qgrd->kgd", grad_scores, queries, preferred_element_type=jnp.float32)
        * score_scale
    )
    return (grad_queries, grad_keys, grad_values)


def per_device_general(
    tokens,
    gain_one,
    gain_two,
    w_query,
    w_key,
    w_value,
    w_out,
    w_gate,
    w_up,
    w_down,
    slot_index,
    slot_gate,
    grad_output,
):
    n_tensor = lax.axis_size("tensor")
    shard_rows, width = tokens.shape
    head_size = HD
    local_heads = w_query.shape[1] // head_size
    local_groups = w_key.shape[0] // head_size
    expert_count, hidden_local, _ = w_gate.shape
    sweeps = math.gcd(expert_count, 4)
    slot_rows = slot_index[0].reshape(sweeps, expert_count // sweeps, -1)
    slot_weight = slot_gate[0].reshape(sweeps, expert_count // sweeps, -1)
    gate_blocks = w_gate.reshape(sweeps, expert_count // sweeps, hidden_local, width)
    up_blocks = w_up.reshape(sweeps, expert_count // sweeps, hidden_local, width)
    down_blocks = w_down.reshape(sweeps, expert_count // sweeps, hidden_local, width)
    row_start = lax.axis_index("tensor") * shard_rows
    full_rows = lax.all_gather(tokens, "tensor", axis=0, tiled=True)
    row_count = full_rows.shape[0]
    seq_count = row_count // SEQ_LEN
    cosine, sine_tab = rope_tables(row_count, head_size)
    rows_float = full_rows.astype(jnp.float32)
    normed_one, inverse_one = normalize(rows_float, gain_one)
    normed_one = normed_one.astype(jnp.bfloat16)
    query_pre = jnp.dot(normed_one, w_query, preferred_element_type=jnp.float32)
    key_pre = jnp.einsum("td,kd->tk", normed_one, w_key, preferred_element_type=jnp.float32)
    values = jnp.einsum(
        "td,kd->tk", normed_one, w_value, preferred_element_type=jnp.float32
    ).astype(jnp.bfloat16)
    queries = rotate(query_pre.reshape(row_count, local_heads, head_size), cosine, sine_tab).astype(
        jnp.bfloat16
    )
    keys = rotate(key_pre.reshape(row_count, local_groups, head_size), cosine, sine_tab).astype(
        jnp.bfloat16
    )
    seq_queries = queries.reshape(
        seq_count, SEQ_LEN, local_groups, local_heads // local_groups, head_size
    )
    seq_keys = keys.reshape(seq_count, SEQ_LEN, local_groups, head_size)
    seq_values = values.reshape(seq_count, SEQ_LEN, local_groups, head_size)
    mixed, log_total = lax.map(attend_forward, (seq_queries, seq_keys, seq_values))
    mixed = mixed.reshape(row_count, local_heads * head_size)
    attn_part = jnp.dot(mixed, w_out, preferred_element_type=jnp.float32)
    attn_shard = lax.psum_scatter(attn_part, "tensor", scatter_dimension=0, tiled=True)
    residual = tokens.astype(jnp.float32) + attn_shard
    normed_shard, inverse_two = normalize(residual, gain_two)
    normed_two = lax.all_gather(normed_shard.astype(jnp.bfloat16), "tensor", axis=0, tiled=True)

    def expert_forward(running, members):
        slot_part, weight_part, gate_part, up_part, down_part = members
        gathered = normed_two[slot_part]
        gate_pre = jnp.einsum(
            "ecd,efd->ecf", gathered, gate_part, preferred_element_type=jnp.float32
        )
        up_pre = jnp.einsum("ecd,efd->ecf", gathered, up_part, preferred_element_type=jnp.float32)
        active = (jax.nn.silu(gate_pre) * up_pre).astype(jnp.bfloat16)
        expert_out = (
            jnp.einsum("ecf,efd->ecd", active, down_part, preferred_element_type=jnp.float32)
            * weight_part[..., None]
        )
        running = running.at[slot_part.reshape(-1)].add(expert_out.reshape(-1, width))
        return (running, ())

    mixture_part, saved = lax.scan(
        expert_forward,
        jnp.zeros((row_count, width), jnp.float32),
        (slot_rows, slot_weight, gate_blocks, up_blocks, down_blocks),
    )
    mixture = lax.psum_scatter(
        mixture_part.astype(jnp.bfloat16), "tensor", scatter_dimension=0, tiled=True
    ).astype(jnp.float32)
    output = (residual + mixture).astype(jnp.bfloat16)
    grad_full = lax.all_gather(grad_output, "tensor", axis=0, tiled=True)

    def expert_backward(running, members):
        slot_part, weight_part, gate_part, up_part, down_part, kept_part = members
        gathered = normed_two[slot_part]
        gate_pre = jnp.einsum(
            "ecd,efd->ecf", gathered, gate_part, preferred_element_type=jnp.float32
        )
        up_pre = jnp.einsum("ecd,efd->ecf", gathered, up_part, preferred_element_type=jnp.float32)
        sigmoid_val = jax.nn.sigmoid(gate_pre)
        silu_val = gate_pre * sigmoid_val
        active = (silu_val * up_pre).astype(jnp.bfloat16)
        grad_out = (grad_full[slot_part].astype(jnp.float32) * weight_part[..., None]).astype(
            jnp.bfloat16
        )
        grad_act = jnp.einsum(
            "ecd,efd->ecf", grad_out, down_part, preferred_element_type=jnp.float32
        )
        grad_gate = (
            grad_act * up_pre * sigmoid_val * (1.0 + gate_pre * (1.0 - sigmoid_val))
        ).astype(jnp.bfloat16)
        grad_up = (grad_act * silu_val).astype(jnp.bfloat16)
        grad_down_w = jnp.einsum(
            "ecf,ecd->efd", active, grad_out, preferred_element_type=jnp.float32
        )
        grad_gate_w = jnp.einsum(
            "ecf,ecd->efd", grad_gate, gathered, preferred_element_type=jnp.float32
        )
        grad_up_w = jnp.einsum(
            "ecf,ecd->efd", grad_up, gathered, preferred_element_type=jnp.float32
        )
        grad_gathered = jnp.einsum(
            "ecf,efd->ecd", grad_gate, gate_part, preferred_element_type=jnp.float32
        )
        grad_gathered = grad_gathered + jnp.einsum(
            "ecf,efd->ecd", grad_up, up_part, preferred_element_type=jnp.float32
        )
        running = running.at[slot_part.reshape(-1)].add(grad_gathered.reshape(-1, width))
        grad_triple = (grad_gate_w, grad_up_w, grad_down_w)
        return (running, grad_triple)

    grad_normed_part, expert_grads = lax.scan(
        expert_backward,
        jnp.zeros((row_count, width), jnp.float32),
        (slot_rows, slot_weight, gate_blocks, up_blocks, down_blocks, saved),
    )
    grad_w_gate = expert_grads[0].reshape(expert_count, hidden_local, width)
    grad_w_up = expert_grads[1].reshape(expert_count, hidden_local, width)
    grad_w_down = expert_grads[2].reshape(expert_count, hidden_local, width)
    shared = (
        lax.psum_scatter(
            grad_w_gate.astype(jnp.bfloat16), "dp", scatter_dimension=2, tiled=True
        ).astype(jnp.float32),
        lax.psum_scatter(
            grad_w_up.astype(jnp.bfloat16), "dp", scatter_dimension=2, tiled=True
        ).astype(jnp.float32),
        lax.psum_scatter(
            grad_w_down.astype(jnp.bfloat16), "dp", scatter_dimension=2, tiled=True
        ).astype(jnp.float32),
    )
    grad_w_gate, grad_w_up, grad_w_down = (
        lax.all_gather(shared[0].astype(jnp.bfloat16), "dp", axis=2, tiled=True).astype(
            jnp.float32
        ),
        lax.all_gather(shared[1].astype(jnp.bfloat16), "dp", axis=2, tiled=True).astype(
            jnp.float32
        ),
        lax.all_gather(shared[2].astype(jnp.bfloat16), "dp", axis=2, tiled=True).astype(
            jnp.float32
        ),
    )
    grad_normed_two = lax.psum_scatter(
        grad_normed_part.astype(jnp.bfloat16), "tensor", scatter_dimension=0, tiled=True
    ).astype(jnp.float32)
    gain_two_part = jnp.sum(grad_normed_two * residual * inverse_two, axis=0)
    grad_resid = grad_output.astype(jnp.float32) + norm_back(
        residual, inverse_two, gain_two, grad_normed_two
    )
    grad_attn = lax.all_gather(grad_resid.astype(jnp.bfloat16), "tensor", axis=0, tiled=True)
    grad_w_out = jnp.dot(mixed.T, grad_attn, preferred_element_type=jnp.float32)
    grad_mixed = jnp.dot(grad_attn, w_out.T, preferred_element_type=jnp.float32).astype(
        jnp.bfloat16
    )
    grad_mixed = grad_mixed.reshape(
        seq_count, SEQ_LEN, local_groups, local_heads // local_groups, head_size
    )
    grad_q_rot, grad_k_rot, grad_v_seq = lax.map(
        attend_backward, (seq_queries, seq_keys, seq_values, grad_mixed, log_total)
    )
    grad_q = unrotate(grad_q_rot.reshape(row_count, local_heads, head_size), cosine, sine_tab)
    grad_q = grad_q.reshape(row_count, local_heads * head_size).astype(jnp.bfloat16)
    grad_k = unrotate(grad_k_rot.reshape(row_count, local_groups, head_size), cosine, sine_tab)
    grad_k = grad_k.reshape(row_count, local_groups * head_size).astype(jnp.bfloat16)
    grad_v = grad_v_seq.reshape(row_count, local_groups * head_size).astype(jnp.bfloat16)
    grad_w_query = jnp.dot(normed_one.T, grad_q, preferred_element_type=jnp.float32)
    grad_w_key = jnp.dot(grad_k.T, normed_one, preferred_element_type=jnp.float32)
    grad_w_value = jnp.dot(grad_v.T, normed_one, preferred_element_type=jnp.float32)
    grad_normed_one = jnp.dot(grad_q, w_query.T, preferred_element_type=jnp.float32)
    grad_normed_one = grad_normed_one + jnp.dot(grad_k, w_key, preferred_element_type=jnp.float32)
    grad_normed_one = grad_normed_one + jnp.dot(grad_v, w_value, preferred_element_type=jnp.float32)
    gain_one_part = jnp.sum(grad_normed_one * rows_float * inverse_one, axis=0)
    gains_tile = jnp.broadcast_to(
        jnp.stack([gain_one_part, gain_two_part])[None], (n_tensor, 2, width)
    )
    grad_normed_shard, gains_sum = (
        lax.psum_scatter(
            grad_normed_one.astype(jnp.bfloat16), "tensor", scatter_dimension=0, tiled=True
        ).astype(jnp.float32),
        lax.psum_scatter(
            gains_tile.astype(jnp.bfloat16), "tensor", scatter_dimension=0, tiled=True
        ).astype(jnp.float32),
    )
    inverse_shard = lax.dynamic_slice_in_dim(inverse_one, row_start, shard_rows, 0)
    grad_input = grad_resid + norm_back(
        tokens.astype(jnp.float32), inverse_shard, gain_one, grad_normed_shard
    )
    grad_tokens = lax.all_gather(grad_input.astype(jnp.bfloat16), "tensor", axis=0, tiled=True)
    grad_w_query, grad_w_key, grad_w_value, grad_w_out, gains_total = (
        lax.psum(grad_w_query.astype(jnp.bfloat16), "dp").astype(jnp.float32),
        lax.psum(grad_w_key.astype(jnp.bfloat16), "dp").astype(jnp.float32),
        lax.psum(grad_w_value.astype(jnp.bfloat16), "dp").astype(jnp.float32),
        lax.psum(grad_w_out.astype(jnp.bfloat16), "dp").astype(jnp.float32),
        lax.psum(gains_sum.astype(jnp.bfloat16), "dp").astype(jnp.float32),
    )
    return (
        output,
        grad_tokens,
        gains_total[0, 0],
        gains_total[0, 1],
        grad_w_query,
        grad_w_key,
        grad_w_value,
        grad_w_out,
        grad_w_gate,
        grad_w_up,
        grad_w_down,
    )


BLOCK = 16
CHUNKS = 4


def nt_dot(left, right):
    return lax.dot_general(
        left, right, (((1,), (1,)), ((), ())), preferred_element_type=jnp.float32
    )


def nn_dot(left, right):
    return lax.dot_general(
        left, right, (((1,), (0,)), ((), ())), preferred_element_type=jnp.float32
    )


def tn_dot(left, right):
    return lax.dot_general(
        left, right, (((0,), (0,)), ((), ())), preferred_element_type=jnp.float32
    )


def expert_body(first, last, experts, cap, rows, width, hidden):
    tiles = width // 128
    shard = rows // 2
    piece = shard // 2

    def body(*refs):
        index_ref, gate_ref, live_ref, place_ref = refs[:4]
        normed_own, normed_other, grad_own, grad_other = refs[4:8]
        gate_w, up_w, down_w = refs[8:11]
        refs = refs[11:]
        if not first:
            mix_in, back_in = refs[:2]
            refs = refs[2:]
        grads_ref = refs[0]
        if last:
            mix_own, mix_other, back_own, back_other = refs[1:5]
            refs = refs[5:]
        else:
            mix_out, back_out = refs[1:3]
            refs = refs[3:]
        (table_n, table_g, sum_m, sum_b, stage_n, stage_g, flat_n, flat_g, sems) = refs
        step = pl.program_id(0)
        place = place_ref[0]

        @pl.when(step == 0)
        def _():
            if not first:
                copy_m = pltpu.make_async_copy(mix_in, sum_m, sems.at[0])
                copy_b = pltpu.make_async_copy(back_in, sum_b, sems.at[1])
                copy_m.start()
                copy_b.start()
            else:
                sum_m[...] = jnp.zeros_like(sum_m)
                sum_b[...] = jnp.zeros_like(sum_b)
            jobs = []
            for part in range(2):
                for half in range(2):
                    jobs.append(
                        (normed_own, normed_other)[part].at[pl.ds(half * piece, piece), :]
                    )
                    jobs.append((grad_own, grad_other)[part].at[pl.ds(half * piece, piece), :])
            flats = (flat_n, flat_g)
            tables = (table_n, table_g)

            def fetch(number):
                kind = number % 2
                return pltpu.make_async_copy(
                    jobs[number], flats[kind].at[pl.ds(0, piece), :], sems.at[2 + kind]
                )

            fetch(0).start()
            fetch(1).start()
            for number in range(8):
                part, half, kind = number // 4, (number // 2) % 2, number % 2
                fetch(number).wait()
                side = place if part == 0 else 1 - place
                base = (side * shard + half * piece) * tiles
                for tile in range(tiles):
                    tables[kind][pl.ds(base + tile, piece, stride=tiles), :] = flats[kind][
                        0:piece, tile * 128 : (tile + 1) * 128
                    ].astype(jnp.float32)
                if number + 2 < 8:
                    fetch(number + 2).start()
            if not first:
                copy_m.wait()
                copy_b.wait()

        blocks = (live_ref[step] + (BLOCK - 1)) // BLOCK
        offset = step * cap

        def gather(block, carry):
            start = block * BLOCK
            for lane in range(BLOCK):
                row = pl.multiple_of(index_ref[offset + start + lane] * tiles, tiles)
                weight = gate_ref[offset + start + lane]
                spot = pl.ds(pl.multiple_of((start + lane) * tiles, tiles), tiles)
                stage_n[spot, :] = table_n[pl.ds(row, tiles), :]
                stage_g[spot, :] = table_g[pl.ds(row, tiles), :] * weight
            return carry

        lax.fori_loop(0, blocks, gather, 0)

        def clear(block, carry):
            spot = pl.ds(pl.multiple_of(block * BLOCK * tiles, BLOCK * tiles), BLOCK * tiles)
            stage_n[spot, :] = jnp.zeros((BLOCK * tiles, 128), jnp.float32)
            stage_g[spot, :] = jnp.zeros((BLOCK * tiles, 128), jnp.float32)
            return carry

        lax.fori_loop(blocks, cap // BLOCK, clear, 0)
        for tile in range(tiles):
            columns = slice(tile * 128, (tile + 1) * 128)
            flat_n[:, columns] = stage_n[pl.ds(tile, cap, stride=tiles), :].astype(jnp.bfloat16)
            flat_g[:, columns] = stage_g[pl.ds(tile, cap, stride=tiles), :].astype(jnp.bfloat16)
        gathered = flat_n[...]
        grad_out = flat_g[...]
        gate_pre = nt_dot(gathered, gate_w[0])
        up_pre = nt_dot(gathered, up_w[0])
        grad_act = nt_dot(grad_out, down_w[0])
        sigmoid_val = jax.nn.sigmoid(gate_pre)
        silu_val = gate_pre * sigmoid_val
        active = (silu_val * up_pre).astype(jnp.bfloat16)
        grad_gate = (
            grad_act * up_pre * sigmoid_val * (1.0 + gate_pre * (1.0 - sigmoid_val))
        ).astype(jnp.bfloat16)
        grad_up = (grad_act * silu_val).astype(jnp.bfloat16)
        expert_out = nn_dot(active, down_w[0])
        grad_rows = nn_dot(grad_gate, gate_w[0]) + nn_dot(grad_up, up_w[0])
        for tile in range(tiles):
            columns = slice(tile * 128, (tile + 1) * 128)
            stage_n[pl.ds(tile, cap, stride=tiles), :] = expert_out[:, columns]
            stage_g[pl.ds(tile, cap, stride=tiles), :] = grad_rows[:, columns]
        middle = hidden // 2
        for kind, (left, right) in enumerate(
            ((grad_gate, gathered), (grad_up, gathered), (active, grad_out))
        ):
            weight_grad = tn_dot(left, right).astype(jnp.bfloat16)
            spot = slice(kind * middle, (kind + 1) * middle)
            grads_ref[0, spot, :] = weight_grad[0:middle]
            grads_ref[1, spot, :] = weight_grad[middle:hidden]

        def scatter(block, carry):
            start = block * BLOCK
            spots, new_m, new_b = [], [], []
            for lane in range(BLOCK):
                row = pl.multiple_of(index_ref[offset + start + lane] * tiles, tiles)
                weight = gate_ref[offset + start + lane]
                spot = pl.ds(pl.multiple_of((start + lane) * tiles, tiles), tiles)
                spots.append(row)
                new_m.append(sum_m[pl.ds(row, tiles), :] + stage_n[spot, :] * weight)
                new_b.append(sum_b[pl.ds(row, tiles), :] + stage_g[spot, :])
            for lane in range(BLOCK):
                sum_m[pl.ds(spots[lane], tiles), :] = new_m[lane]
                sum_b[pl.ds(spots[lane], tiles), :] = new_b[lane]
            return carry

        lax.fori_loop(0, blocks, scatter, 0)

        @pl.when(step == experts - 1)
        def _():
            if not last:
                copy_m = pltpu.make_async_copy(sum_m, mix_out, sems.at[0])
                copy_b = pltpu.make_async_copy(sum_b, back_out, sems.at[1])
                copy_m.start()
                copy_b.start()
                copy_m.wait()
                copy_b.wait()
            else:
                sums = (sum_b, sum_m)
                flats = (flat_g, flat_n)
                targets = ((back_other, mix_other), (back_own, mix_own))

                def put(number):
                    part, half, kind = number // 4, (number // 2) % 2, number % 2
                    return pltpu.make_async_copy(
                        flats[kind].at[pl.ds(0, piece), :],
                        targets[part][kind].at[pl.ds(half * piece, piece), :],
                        sems.at[2 + kind],
                    )

                for number in range(8):
                    part, half, kind = number // 4, (number // 2) % 2, number % 2
                    if number >= 2:
                        put(number - 2).wait()
                    side = 1 - place if part == 0 else place
                    base = (side * shard + half * piece) * tiles
                    for tile in range(tiles):
                        flats[kind][0:piece, tile * 128 : (tile + 1) * 128] = sums[kind][
                            pl.ds(base + tile, piece, stride=tiles), :
                        ].astype(jnp.bfloat16)
                    put(number).start()
                put(6).wait()
                put(7).wait()

    return body


def expert_chunk(first, last, number, place, index, weights, live, tables, params, sums):
    experts = index.shape[0]
    cap = index.shape[1]
    shard, width = tables[0].shape
    rows = 2 * shard
    hidden = params[0].shape[1]
    tiles = width // 128
    any_spec = pl.BlockSpec(memory_space=pl.ANY)

    def weight_map(step, *_):
        return (number * experts + step, 0, 0)

    def grads_map(step, *_):
        return (step, 0, 0)

    weight_spec = pl.BlockSpec((1, hidden, width), weight_map)
    in_specs = [any_spec] * 4 + [weight_spec] * 3
    operands = list(tables) + list(params)
    if not first:
        in_specs = in_specs + [any_spec] * 2
        operands = operands + list(sums)
    unit_rows = 3 * hidden // 2
    out_specs = [pl.BlockSpec((2, unit_rows, width), grads_map)]
    out_shape = [jax.ShapeDtypeStruct((2 * experts, unit_rows, width), jnp.bfloat16)]
    aliases = {}
    if last:
        out_specs = out_specs + [any_spec] * 4
        out_shape = out_shape + [jax.ShapeDtypeStruct((shard, width), jnp.bfloat16)] * 4
    else:
        out_specs = out_specs + [any_spec] * 2
        out_shape = out_shape + [jax.ShapeDtypeStruct((rows * tiles, 128), jnp.float32)] * 2
    flops = 18 * experts * cap * hidden * width
    return pl.pallas_call(
        expert_body(first, last, experts, cap, rows, width, hidden),
        grid_spec=pltpu.PrefetchScalarGridSpec(
            num_scalar_prefetch=4,
            grid=(experts,),
            in_specs=in_specs,
            out_specs=out_specs,
            scratch_shapes=[
                pltpu.VMEM((rows * tiles, 128), jnp.float32),
                pltpu.VMEM((rows * tiles, 128), jnp.float32),
                pltpu.VMEM((rows * tiles, 128), jnp.float32),
                pltpu.VMEM((rows * tiles, 128), jnp.float32),
                pltpu.VMEM((cap * tiles, 128), jnp.float32),
                pltpu.VMEM((cap * tiles, 128), jnp.float32),
                pltpu.VMEM((cap, width), jnp.bfloat16),
                pltpu.VMEM((cap, width), jnp.bfloat16),
                pltpu.SemaphoreType.DMA((4,)),
            ],
        ),
        out_shape=out_shape,
        input_output_aliases=aliases,
        compiler_params=pltpu.CompilerParams(
            dimension_semantics=("arbitrary",), vmem_limit_bytes=60 * 1024 * 1024
        ),
        cost_estimate=pl.CostEstimate(
            flops=flops, transcendentals=0, bytes_accessed=12 * experts * hidden * width + 40 * rows * width
        ),
        name="experts",
    )(index.reshape(-1), weights.reshape(-1), live, place, *operands)


def add_bf16(left, right):
    return (left.astype(jnp.float32) + right.astype(jnp.float32)).astype(jnp.bfloat16)


def sum_over_dp(units):
    devices = lax.axis_size("dp")
    depth = devices // 4
    me = lax.axis_index("dp")
    core, row, level = me % 2, (me // 2) % 2, me // 4
    over_core = [(i, i ^ 1) for i in range(devices)]
    over_row = [(i, i ^ 2) for i in range(devices)]
    up = [(i, i + 4) for i in range(devices - 4)]
    down = [(i + 4, i) for i in range(devices - 4)]
    send = lambda value, pairs: lax.ppermute(value, "dp", pairs)
    take = lambda value, start, size: lax.dynamic_slice_in_dim(value, start, size, 0)
    half = devices // 2
    got = send(take(units, (1 - core) * half, half), over_core)
    units = add_bf16(take(units, core * half, half), got)
    got = send(take(units, (1 - row) * depth, depth), over_row)
    units = add_bf16(take(units, row * depth, depth), got)
    got_up = got_down = None
    for step in range(1, depth):
        part_up = take(units, jnp.minimum(depth + level - step, depth - 1), 1)
        part_down = take(units, jnp.maximum(level + step - depth, 0), 1)
        if step > 1:
            part_up = add_bf16(part_up, got_up)
            part_down = add_bf16(part_down, got_down)
        got_up = send(part_up, up)
        got_down = send(part_down, down)
    mine = (
        take(units, level, 1).astype(jnp.float32)
        + got_up.astype(jnp.float32)
        + got_down.astype(jnp.float32)
    ).astype(jnp.bfloat16)
    ups, downs = [mine], [mine]
    for step in range(1, depth):
        ups.append(send(ups[-1], up))
        downs.append(send(downs[-1], down))
    line = [mine] + [
        jnp.where(level >= step, ups[step], downs[depth - step]) for step in range(1, depth)
    ]
    line = jnp.concatenate(line, axis=0)
    plane = jnp.concatenate([line, send(line, over_row)], axis=0)
    return plane, send(plane, over_core)


def spread(number, chunks, spot, parts, earlier):
    half, unit_rows, width = parts[0].shape
    middle = unit_rows // 3
    depth = half // 2
    experts = half

    def body(spot_ref, mine_ref, other_ref, *refs):
        outs = refs[-3:]

        @pl.when(pl.program_id(0) < half)
        def _():
            for kind in range(3):
                outs[kind][0] = mine_ref[0, kind * middle : (kind + 1) * middle, :].astype(
                    jnp.float32
                )

        @pl.when(pl.program_id(0) >= half)
        def _():
            for kind in range(3):
                outs[kind][0] = other_ref[0, kind * middle : (kind + 1) * middle, :].astype(
                    jnp.float32
                )

    def out_map(step, spot_ref):
        core = jnp.where(step >= half, 1 - spot_ref[0], spot_ref[0])
        inside = lax.rem(step, half)
        row = jnp.where(inside >= depth, 1 - spot_ref[1], spot_ref[1])
        level = lax.rem(spot_ref[2] + depth - lax.rem(inside, depth), depth)
        unit = core * half + row * depth + level
        return (number * experts + unit // 2, lax.rem(unit, 2), 0)

    out_spec = pl.BlockSpec((1, middle, width), out_map)
    in_specs = [
        pl.BlockSpec((1, unit_rows, width), lambda step, _: (jnp.minimum(step, half - 1), 0, 0)),
        pl.BlockSpec((1, unit_rows, width), lambda step, _: (jnp.maximum(step - half, 0), 0, 0)),
    ]
    operands = list(parts)
    aliases = {}
    if earlier is not None:
        in_specs = in_specs + [pl.BlockSpec(memory_space=pl.ANY)] * 3
        operands = operands + list(earlier)
        aliases = {3: 0, 4: 1, 5: 2}
    return pl.pallas_call(
        body,
        grid_spec=pltpu.PrefetchScalarGridSpec(
            num_scalar_prefetch=1,
            grid=(2 * half,),
            in_specs=in_specs,
            out_specs=[out_spec] * 3,
        ),
        out_shape=[jax.ShapeDtypeStruct((chunks * experts, 2 * middle, width), jnp.float32)] * 3,
        input_output_aliases=aliases,
        compiler_params=pltpu.CompilerParams(dimension_semantics=("arbitrary",)),
        cost_estimate=pl.CostEstimate(
            flops=0, transcendentals=0, bytes_accessed=12 * half * unit_rows * width
        ),
        name="spread",
    )(spot, *operands)


def per_device_pair(
    tokens,
    gain_one,
    gain_two,
    w_query,
    w_key,
    w_value,
    w_out,
    w_gate,
    w_up,
    w_down,
    slot_index,
    slot_gate,
    grad_output,
):
    rows, width = tokens.shape
    experts, hidden, _ = w_gate.shape
    swap = lambda value: lax.ppermute(value, "tensor", [(0, 1), (1, 0)])
    place = lax.axis_index("tensor").astype(jnp.int32)
    cosine, sine_tab = rope_tables(rows, HD)
    w_other = [swap(value) for value in (w_query, w_key, w_value)]
    grad_other = swap(grad_output)
    out_other = swap(w_out)
    rows_float = tokens.astype(jnp.float32)
    normed_one, inverse_one = normalize(rows_float, gain_one)
    normed_one = normed_one.astype(jnp.bfloat16)

    def heads_forward(query_w, key_w, value_w):
        groups = key_w.shape[0] // HD
        heads = query_w.shape[1] // HD
        query_pre = jnp.dot(normed_one, query_w, preferred_element_type=jnp.float32)
        key_pre = nt_dot(normed_one, key_w)
        values = nt_dot(normed_one, value_w).astype(jnp.bfloat16).reshape(rows, groups, HD)
        queries = rotate(query_pre.reshape(rows, heads, HD), cosine, sine_tab)
        queries = queries.astype(jnp.bfloat16).reshape(rows, groups, heads // groups, HD)
        keys = rotate(key_pre.reshape(rows, groups, HD), cosine, sine_tab).astype(jnp.bfloat16)
        mixed, log_total = attend_forward((queries, keys, values))
        return (queries, keys, values, mixed.reshape(rows, heads * HD), log_total)

    own = heads_forward(w_query, w_key, w_value)
    other = heads_forward(*w_other)
    residual = (
        rows_float
        + jnp.dot(own[3], w_out, preferred_element_type=jnp.float32)
        + jnp.dot(other[3], out_other, preferred_element_type=jnp.float32)
    )
    normed_two, inverse_two = normalize(residual, gain_two)
    normed_two = normed_two.astype(jnp.bfloat16)
    normed_other = swap(normed_two)

    index = slot_index[0]
    weights = slot_gate[0]
    live = jnp.sum((weights > 0.0).astype(jnp.int32), axis=1)
    chunks = math.gcd(experts, CHUNKS)
    per_chunk = experts // chunks
    sums = None
    summed = []
    for number in range(chunks):
        part = slice(number * per_chunk, (number + 1) * per_chunk)
        result = expert_chunk(
            number == 0,
            number == chunks - 1,
            number,
            place[None],
            index[part],
            weights[part],
            live[part],
            (normed_two, normed_other, grad_output, grad_other),
            (w_gate, w_up, w_down),
            sums,
        )
        summed.append(sum_over_dp(result[0]))
        sums = result[1:]
    me = lax.axis_index("dp").astype(jnp.int32)
    spot = jnp.stack([me % 2, (me // 2) % 2, me // 4])
    expert_grads = None
    for number in range(chunks):
        expert_grads = spread(number, chunks, spot, summed[number], expert_grads)
    mix_own, mix_other, back_own, back_other = sums
    grad_normed_two = back_own.astype(jnp.float32) + swap(back_other).astype(jnp.float32)
    output = (
        residual + mix_own.astype(jnp.float32) + swap(mix_other).astype(jnp.float32)
    ).astype(jnp.bfloat16)
    gain_two_part = jnp.sum(grad_normed_two * residual * inverse_two, axis=0)
    grad_resid = grad_output.astype(jnp.float32) + norm_back(
        residual, inverse_two, gain_two, grad_normed_two
    )
    grad_attn = grad_resid.astype(jnp.bfloat16)

    def heads_backward(saved, query_w, key_w, value_w, out_w):
        queries, keys, values, mixed, log_total = saved
        groups = keys.shape[1]
        heads = queries.shape[1] * queries.shape[2]
        out_grad = tn_dot(mixed, grad_attn)
        grad_mixed = nt_dot(grad_attn, out_w).astype(jnp.bfloat16)
        grad_q, grad_k, grad_v = attend_backward(
            (queries, keys, values, grad_mixed.reshape(queries.shape), log_total)
        )
        grad_q = unrotate(grad_q.reshape(rows, heads, HD), cosine, sine_tab)
        grad_q = grad_q.reshape(rows, heads * HD).astype(jnp.bfloat16)
        grad_k = unrotate(grad_k, cosine, sine_tab)
        grad_k = grad_k.reshape(rows, groups * HD).astype(jnp.bfloat16)
        grad_v = grad_v.reshape(rows, groups * HD).astype(jnp.bfloat16)
        weight_grads = (
            tn_dot(normed_one, grad_q),
            tn_dot(grad_k, normed_one),
            tn_dot(grad_v, normed_one),
            out_grad,
        )
        back = nt_dot(grad_q, query_w) + nn_dot(grad_k, key_w) + nn_dot(grad_v, value_w)
        return (weight_grads, back)

    theirs, back_two = heads_backward(other, *w_other, out_other)
    mine, back_one = heads_backward(own, w_query, w_key, w_value, w_out)
    grad_normed_one = back_one + back_two
    gain_one_part = jnp.sum(grad_normed_one * rows_float * inverse_one, axis=0)
    grad_input = (
        grad_resid + norm_back(rows_float, inverse_one, gain_one, grad_normed_one)
    ).astype(jnp.bfloat16)
    input_other = swap(grad_input)
    grad_tokens = jnp.where(
        place == 0,
        jnp.concatenate([grad_input, input_other], axis=0),
        jnp.concatenate([input_other, grad_input], axis=0),
    )
    weight_grads = [
        lax.psum(
            (left + swap(right.astype(jnp.bfloat16)).astype(jnp.float32)).astype(jnp.bfloat16),
            "dp",
        ).astype(jnp.float32)
        for left, right in zip(mine, theirs)
    ]
    gains = lax.psum(jnp.stack([gain_one_part, gain_two_part]), ("dp", "tensor"))
    return (
        output,
        grad_tokens,
        gains[0],
        gains[1],
        *weight_grads,
        *expert_grads,
    )


def per_device(*operands):
    rows = operands[0].shape[0]
    experts = operands[7].shape[0]
    fits = 2 * experts == CHUNKS * lax.axis_size("dp") and lax.axis_size("dp") % 8 == 0
    if lax.axis_size("tensor") == 2 and rows == SEQ_LEN and fits:
        return per_device_pair(*operands)
    return per_device_general(*operands)


def solution(mesh):
    placed = (
        P(("dp", "tensor"), None),
        P(),
        P(),
        P(None, "tensor"),
        P("tensor", None),
        P("tensor", None),
        P("tensor", None),
        P(None, "tensor", None),
        P(None, "tensor", None),
        P(None, "tensor", None),
        P("dp", None, None),
        P("dp", None, None),
        P(("dp", "tensor"), None),
    )
    return jax.shard_map(
        per_device,
        mesh=mesh,
        in_specs=placed,
        out_specs=(
            P(("dp", "tensor"), None),
            P("dp", None),
            P(),
            P(),
            P(None, "tensor"),
            P("tensor", None),
            P("tensor", None),
            P("tensor", None),
            P(None, "tensor", None),
            P(None, "tensor", None),
            P(None, "tensor", None),
        ),
        check_vma=False,
    )
```
